32 devices in a mesh: occ: 4 (over z), virt: 8 (over y, x, core).
Axes of the slice: x: 2, y: 2, z: 4, core: 2. Of those that a mesh axis runs over, the one named last changes fastest.
Arguments:
- amplitudes: float32 [128, 8192], P('occ', 'virt'), may hold values from -6 to 6
- tiles: float32 [2048, 128, 128], P(('occ', 'virt')), may hold values from -0.15625 to 0.15625
- tile_code: int32 [2048], P(('occ', 'virt')), may hold values from 0 to 127, as said below
- tile_count: int32 [32], P(('occ', 'virt')), may hold values from 16 to 64, as said below
- occ_energy: float32 [128], P('virt'), may hold values from -3 to -0.5
- virt_energy: float32 [8192], P('occ'), may hold values from 1 to 4
Outputs:
- updated: float32 [128, 8192], P('virt', 'occ')
The draws below stay inside these ranges and needn't reach their ends.
Inputs may be any that keep to these rules, and one draw needn't show every extreme that they name: `tile_code`: within one device's 64 slots the positions are distinct. `tile_count`: some device has all 64 slots live.
All inputs are finite; a program needn't handle non-finite values.
Results may differ from the reference program's by a relative error of at most 0.0003.
Values sent between devices are 32-bit elements; how exact they have to be, the bound alone decides.
A program may use at most 64 MiB of HBM per device.

```python
import jax
import jax.numpy as jnp
from jax import lax

TILE = 128
VP_DEV = 1024
AB_DEV = 2048
NNZ_DEV = 64
OP = 128
VP = 8192
GRID = 128
NNZ_ALL = 2048
N_VIRT = 8


def draw_tile_code(key, part):
    devices = NNZ_ALL // NNZ_DEV
    subkeys = jax.random.split(jax.random.fold_in(key, 11), devices)
    tile_codes = jax.vmap(lambda single: jax.random.permutation(single, GRID)[:NNZ_DEV])(subkeys)
    return tile_codes.reshape(-1).astype(jnp.int32)


def draw_tile_count(key, part):
    devices = NNZ_ALL // NNZ_DEV
    first, second = jax.random.split(jax.random.fold_in(key, 13))
    counts = jax.random.randint(first, (devices,), NNZ_DEV // 4, NNZ_DEV // 2 + 1)
    busiest = jax.random.randint(second, (), 0, devices)
    return jnp.where(jnp.arange(devices) == busiest, NNZ_DEV, counts).astype(jnp.int32)


def level_of(stream_key, extent, cuts, low, largest):
    loudness, own = 1.0, jax.random.fold_in(stream_key, 6)
    for axis_at, parts in cuts:
        steps = jnp.exp(jax.random.uniform(jax.random.fold_in(own, axis_at), (parts,), jnp.float32, low / len(cuts), largest / len(cuts)))
        loudness = loudness * jnp.repeat(steps, extent[axis_at] // parts).reshape([-1 if axis == axis_at else 1 for axis in range(len(extent))])
    return loudness


def bell_draw(own_key, extent, scale, bound, cuts=(), held_as=jnp.bfloat16):
    values = scale * jax.random.normal(own_key, extent, jnp.float32)
    if cuts:
        values = values * level_of(own_key, extent, cuts, -0.22, 0.18)
    return jnp.clip(values, -bound, bound).astype(held_as)


def setup_inputs(seed: int = 0) -> dict:
    streams_of = jax.random.split(jax.random.key(seed), 7)
    return {
        "amplitudes": bell_draw(streams_of[0], (OP, VP), 1.0, 6.0, ((0, 4), (1, 8)), jnp.float32),
        "tiles": bell_draw(streams_of[1], (NNZ_ALL, TILE, TILE), (VP // 6) ** -0.5, 0.15625, ((0, 32),), jnp.float32),
        "tile_code": draw_tile_code(jax.random.fold_in(streams_of[6], 71), 0),
        "tile_count": draw_tile_count(jax.random.fold_in(streams_of[6], 71), 0),
        "occ_energy": jnp.clip(-3.0 + 2.5 * jax.random.uniform(streams_of[4], (OP,), jnp.float32) ** level_of(streams_of[4], (OP,), ((0, 8),), -0.2, 0.2), -3.0, -0.5),
        "virt_energy": jnp.clip(1.0 + 3.0 * jax.random.uniform(streams_of[5], (VP,), jnp.float32) ** level_of(streams_of[5], (VP,), ((0, 4),), -0.2, 0.2), 1.0, 4.0),
    }


def reference(amplitudes, tiles, tile_code, tile_count, occ_energy, virt_energy):
    row_tiles = VP_DEV // TILE
    col_tiles = AB_DEV // TILE
    slots = jnp.arange(NNZ_ALL, dtype=jnp.int32)
    device = slots // NNZ_DEV
    within = slots % NNZ_DEV
    occ_index = device // N_VIRT
    virt_index = device % N_VIRT
    live = within < tile_count[device]
    row_start = ((virt_index * row_tiles + tile_code // col_tiles) * TILE).astype(jnp.int32)
    col_start = ((occ_index * col_tiles + tile_code % col_tiles) * TILE).astype(jnp.int32)

    def add_tile(total, item):
        rstart, cstart, flag, block = item

        def apply(current):
            columns = lax.dynamic_slice_in_dim(amplitudes, rstart, TILE, 1)
            term = jnp.dot(columns, block, precision=lax.Precision.HIGHEST, preferred_element_type=jnp.float32)
            present = lax.dynamic_slice_in_dim(current, cstart, TILE, 1)
            return lax.dynamic_update_slice_in_dim(current, present + term, cstart, 1)

        return lax.cond(flag, apply, lambda current: current, total), None

    start = jnp.zeros((OP, VP), jnp.float32)
    ladder, _ = lax.scan(add_tile, start, (row_start, col_start, live, tiles))
    return ladder / (virt_energy[None, :] - occ_energy[:, None])
```

```python
import functools

import jax
import jax.numpy as jnp
from jax import lax
from jax.experimental import pallas as pl
from jax.experimental.pallas import tpu as pltpu
from jax.sharding import PartitionSpec as P

MESH = pl.DeviceIdType.MESH
TAIL = 1
CHUNKS = 4
REACHES = (2, 2)
GRANT = 50 * 2**20


def flip(index, mask, size):
    out = index * 0
    bit = 1
    while bit < size:
        digit = lax.rem(lax.div(index, bit), 2)
        if mask & bit:
            digit = 1 - digit
        out = out + digit * bit
        bit *= 2
    return out


def kernel(
    no, nv, reaches,
    code_in, count_in, occ_in, virt_in, amp_in, tiles_in, out_ref,
    code, count, occ_energy, virt_energy, slot_map, slot_of,
    tiles, high, low, amps, lhss, parts, partner_parts, summeds, arriveds, own_tail, stage,
    small_sem, slot_sem, tile_sem, own_sem, next_in, plane_in,
    gather_send, gather_recv, core_send, core_recv, chip_send, chip_recv,
):
    o = lax.axis_index("occ")
    v = lax.axis_index("virt")
    core = lax.rem(v, 2)
    chip = lax.div(v, 2)
    chips = nv // 2
    depth = amp_in.shape[-1]
    tile = tiles_in.shape[1]
    dest, width = out_ref.shape
    pairs = amp_in.shape[0]
    reach = max(reaches)
    phases = len(amps)
    levels = [summed.shape[1] for summed in summeds]
    starts = [sum(levels[:phase]) for phase in range(phases)]
    col_tiles = width // tile
    positions = (depth // tile) * col_tiles
    slots = tiles_in.shape[0]
    other_core = (o, v + 1 - 2 * core)

    small = [
        pltpu.make_async_copy(source, target, small_sem.at[number])
        for number, (source, target) in enumerate(
            ((code_in, code), (count_in, count), (occ_in, occ_energy), (virt_in, virt_energy))
        )
    ]
    own_copies = [
        pltpu.make_async_copy(amp_in.at[:, :, 1], own_tail, own_sem.at[1]),
        pltpu.make_async_copy(amp_in.at[:, :, 0], amps[0].at[o], own_sem.at[0]),
    ]
    tile_copy = pltpu.make_async_copy(tiles_in, tiles.at[pl.ds(0, slots)], tile_sem)

    barrier = pltpu.get_barrier_semaphore()

    def meet(device):
        pl.semaphore_signal(barrier, inc=1, device_id=device, device_id_type=MESH)

    for hop in range(1, reach + 1):

        @pl.when(o + hop < no)
        def _():
            meet((o + hop, v))

    def one(condition):
        return condition.astype(jnp.int32)

    before = one(core == 1)
    after = one(core == 0)
    for mask in range(1, chips):
        there = flip(chip, mask, chips)
        before = before + one(there < chip)
        after = after + one(there > chip)

        @pl.when(there > chip)
        def _():
            meet((o, 2 * there + core))

    @pl.when(core == 0)
    def _():
        meet(other_core)

    own_copies[0].start()
    for copy in small:
        copy.start()
    own_copies[1].start()
    tile_copy.start()

    for hop in range(1, reach + 1):
        before = before + one(o >= hop)

    @pl.when(before > 0)
    def _():
        pl.semaphore_wait(barrier, before)

    for hop in range(1, reach + 1):

        @pl.when(o >= hop)
        def _():
            pl.semaphore_signal(
                next_in.at[hop - 1], inc=1, device_id=(o - hop, v), device_id_type=MESH
            )

    def gather_copy(which, phase, hop, side, source=None):
        held = amps[phase].at[which]
        return pltpu.make_async_remote_copy(
            src_ref=held if source is None else source,
            dst_ref=held,
            send_sem=gather_send.at[side, which, hop - 1, phase],
            recv_sem=gather_recv.at[which, phase],
            device_id=(o + hop * (2 * side - 1), v),
            device_id_type=MESH,
        )

    def exists(hop, side):
        return o + hop < no if side else o >= hop

    def send_own(phase, hop, side):
        @pl.when(exists(hop, side))
        def _():
            gather_copy(o, phase, hop, side, amp_in.at[:, :, 0] if phase == 0 else None).start()

    for hop in range(reaches[0], 0, -1):
        send_own(0, hop, 0)

    for mask in range(1, chips):
        there = flip(chip, mask, chips)

        @pl.when(there < chip)
        def _():
            pl.semaphore_signal(
                plane_in, inc=1, device_id=(o, 2 * there + core), device_id_type=MESH
            )

    @pl.when(core == 1)
    def _():
        pl.semaphore_signal(plane_in, inc=1, device_id=other_core, device_id_type=MESH)

    own_copies[0].wait()
    for phase in range(1, phases):
        level = levels[phase]
        for pair in range(pairs):
            for side in range(2):
                amps[phase][o, pair, pl.ds(side * level, level)] = own_tail[
                    pair, side, pl.ds((phase - 1) * level, level)
                ]
        for hop in range(reaches[phase], 0, -1):
            send_own(phase, hop, 0)

    tiles[slots] = jnp.zeros(tiles.shape[1:], tiles.dtype)
    small[0].wait()
    small[1].wait()
    lanes = slot_map.shape[1]
    place_index = lax.broadcasted_iota(jnp.int32, slot_map.shape, 0) * lanes + (
        lax.broadcasted_iota(jnp.int32, slot_map.shape, 1)
    )
    found = jnp.full(slot_map.shape, slots, jnp.int32)
    live = count[0]
    for slot in range(slots):
        found = jnp.where(place_index == jnp.where(slot < live, code[slot], -1), slot, found)
    slot_map[...] = found
    slot_copy = pltpu.make_async_copy(slot_map, slot_of, slot_sem)
    slot_copy.start()

    def place(position, carry):
        value = tiles[slot_of[lax.div(position, lanes), lax.rem(position, lanes)]]
        rounded = value.astype(jnp.bfloat16)
        at_row = pl.multiple_of(lax.div(position, col_tiles) * tile, tile)
        at_col = pl.multiple_of(lax.rem(position, col_tiles) * tile, tile)
        high[pl.ds(at_row, tile), pl.ds(at_col, tile)] = rounded
        low[pl.ds(at_row, tile), pl.ds(at_col, tile)] = (
            value - rounded.astype(jnp.float32)
        ).astype(jnp.bfloat16)
        return carry

    for hop in range(1, reach + 1):

        @pl.when(exists(hop, 1))
        def _():
            pl.semaphore_wait(next_in.at[hop - 1], 1)

        for phase in range(phases):
            if hop <= reaches[phase]:
                send_own(phase, hop, 1)
        if hop == 1:
            tile_copy.wait()
            slot_copy.wait()
        lax.fori_loop(
            positions * (hop - 1) // reach, positions * hop // reach, place, 0
        )
    own_copies[1].wait()

    def relay(phase, distance):
        for side in range(2):

            @pl.when(exists(distance, 1 - side) & exists(1, side))
            def _():
                which = o + distance * (1 - 2 * side)
                gather_copy(which, phase, 1, side).wait_recv()
                for hop in range(reaches[phase], 0, -1):

                    @pl.when(exists(hop, side))
                    def _():
                        gather_copy(which, phase, hop, side).start()

    def arrive(phase, distance):
        for side in range(2):
            here = exists(distance, 1 - side)
            if distance % reaches[phase] == 0 and distance < no - 1:
                here = here & jnp.logical_not(exists(1, side))

            @pl.when(here)
            def _():
                gather_copy(o + distance * (1 - 2 * side), phase, 1, side).wait_recv()

    chunk = width // CHUNKS

    def split(phase):
        rows = lhss[phase].shape[0] // 2
        half = rows // 2
        level = levels[phase]
        if phase:
            for which in range(no):
                for pair in range(pairs):
                    for side in range(2):
                        stage[pl.ds(side * half + (which * pairs + pair) * level, level)] = amps[
                            phase
                        ][which, pair, pl.ds(side * level, level)]
        for side in range(2):
            if phase:
                value = stage[pl.ds(side * half, half)]
            else:
                value = amps[0][:, :, side].reshape(half, depth)
            rounded = value.astype(jnp.bfloat16)
            lhss[phase][pl.ds(side * half, half)] = rounded
            lhss[phase][pl.ds(rows + side * half, half)] = (
                value - rounded.astype(jnp.float32)
            ).astype(jnp.bfloat16)

    def core_copy(phase, at):
        cols = pl.ds(at * chunk, chunk)
        return pltpu.make_async_remote_copy(
            src_ref=parts[phase].at[1 - core, :, cols],
            dst_ref=partner_parts[phase].at[:, cols],
            send_sem=core_send.at[phase, at],
            recv_sem=core_recv.at[phase, at],
            device_id=other_core,
            device_id_type=MESH,
        )

    def chip_copy(phase, mask, at):
        cols = pl.ds(at * chunk, chunk)
        there = flip(chip, mask, chips)
        return pltpu.make_async_remote_copy(
            src_ref=summeds[phase].at[there, :, cols],
            dst_ref=arriveds[phase].at[mask - 1, :, cols],
            send_sem=chip_send.at[phase, mask - 1, at],
            recv_sem=chip_recv.at[phase, mask - 1, at],
            device_id=(o, 2 * there + core),
            device_id_type=MESH,
        )

    def multiply(phase, at):
        rows = lhss[phase].shape[0] // 2
        cols = pl.ds(at * chunk, chunk)
        wide = jnp.dot(lhss[phase][...], high[:, cols], preferred_element_type=jnp.float32)
        narrow = jnp.dot(
            lhss[phase][pl.ds(0, rows)], low[:, cols], preferred_element_type=jnp.float32
        )
        total = wide[:rows] + (wide[rows:] + narrow)
        parts[phase][:, :, cols] = total.reshape(2, rows // 2, chunk)
        core_copy(phase, at).start()

    def pass_on(phase, at):
        level = levels[phase]
        cols = pl.ds(at * chunk, chunk)
        core_copy(phase, at).wait_recv()
        for there in range(chips):
            rows = pl.ds(there * level, level)
            summeds[phase][there, :, cols] = (
                parts[phase][core, rows, cols] + partner_parts[phase][rows, cols]
            )
        for mask in range(chips - 1, 0, -1):
            chip_copy(phase, mask, at).start()

    for distance in range(1, no):
        for phase in range(phases):
            if distance % reaches[phase] == 0 and distance < no - 1:
                relay(phase, distance)

    for phase in range(phases):
        for distance in range(1, no):
            arrive(phase, distance)
        split(phase)
        if phase == 0:

            @pl.when(after > 0)
            def _():
                pl.semaphore_wait(plane_in, after)

        for at in range(CHUNKS):
            multiply(phase, at)
            if at > 1:
                pass_on(phase, at - 2)
        for at in range(max(CHUNKS - 2, 0), CHUNKS):
            pass_on(phase, at)

    small[2].wait()
    small[3].wait()
    for phase in range(phases):
        level = levels[phase]
        shape = (level, chunk)
        row_index = lax.broadcasted_iota(jnp.int32, shape, 0)
        energy = jnp.zeros(shape, jnp.float32)
        for row in range(level):
            energy = jnp.where(row_index == row, occ_energy[starts[phase] + row], energy)
        for at in range(CHUNKS):
            cols = pl.ds(at * chunk, chunk)
            total = summeds[phase][chip, :, cols]
            for mask in range(1, chips):
                chip_copy(phase, mask, at).wait_recv()
                total = total + arriveds[phase][mask - 1, :, cols]
            out_ref[pl.ds(starts[phase], level), cols] = total / (virt_energy[:, cols] - energy)

    for phase in range(phases):
        for at in range(CHUNKS):
            core_copy(phase, at).wait_send()
            for mask in range(1, chips):
                chip_copy(phase, mask, at).wait_send()
        for side in range(2):
            for distance in range(0, no, reaches[phase]):

                @pl.when(exists(distance, 1 - side))
                def _():
                    which = o + distance * (1 - 2 * side)
                    for hop in range(1, reaches[phase] + 1):

                        @pl.when(exists(hop, side))
                        def _():
                            gather_copy(which, phase, hop, side).wait_send()


def body(no, nv, amplitudes, tiles, tile_code, tile_count, occ_energy, virt_energy):
    block, depth = amplitudes.shape
    slots, tile, _ = tiles.shape
    width = virt_energy.shape[0]
    dest = occ_energy.shape[0]
    chips = nv // 2
    top = dest // 2
    levels = [top] + [(dest - top) // TAIL] * TAIL
    phases = len(levels)
    pairs = block // (2 * dest)
    reaches = REACHES if no <= 4 else (1,) * phases
    reach = max(reaches)
    map_shape = (max(8, (depth // tile) * (width // tile) // 128), 128)
    f32, bf16, i32 = jnp.float32, jnp.bfloat16, jnp.int32
    vmem, smem, dma = pltpu.VMEM, pltpu.SMEM, pltpu.SemaphoreType.DMA
    regular = pltpu.SemaphoreType.REGULAR
    return pl.pallas_call(
        functools.partial(kernel, no, nv, reaches),
        out_shape=jax.ShapeDtypeStruct((dest, width), f32),
        in_specs=[pl.BlockSpec(memory_space=pltpu.HBM)] * 6,
        out_specs=pl.BlockSpec(memory_space=pltpu.VMEM),
        scratch_shapes=[
            smem(tile_code.shape, i32),
            smem(tile_count.shape, i32),
            smem((dest,), f32),
            vmem((1, width), f32),
            vmem(map_shape, i32),
            smem(map_shape, i32),
            vmem((slots + 1, tile, tile), f32),
            vmem((depth, width), bf16),
            vmem((depth, width), bf16),
            [vmem((no, pairs, 2, top, depth), f32)]
            + [vmem((no, pairs, 2 * level, depth), f32) for level in levels[1:]],
            [vmem((4 * chips * level, depth), bf16) for level in levels],
            [vmem((2, chips * level, width), f32) for level in levels],
            [vmem((chips * level, width), f32) for level in levels],
            [vmem((chips, level, width), f32) for level in levels],
            [vmem((chips - 1, level, width), f32) for level in levels],
            vmem((pairs, 2, dest - top, depth), f32),
            vmem((2 * chips * levels[-1], depth), f32),
            dma((4,)),
            dma,
            dma,
            dma((2,)),
            regular((reach,)),
            regular,
            dma((2, no, reach, phases)),
            dma((no, phases)),
            dma((phases, CHUNKS)),
            dma((phases, CHUNKS)),
            dma((phases, chips - 1, CHUNKS)),
            dma((phases, chips - 1, CHUNKS)),
        ],
        compiler_params=pltpu.CompilerParams(
            collective_id=0, has_side_effects=True, vmem_limit_bytes=GRANT
        ),
    )(
        *(
            a if a is tile_count else pltpu.with_memory_space_constraint(a, pltpu.HBM)
            for a in (
                tile_code,
                tile_count,
                occ_energy,
                virt_energy.reshape(1, width),
                amplitudes.reshape(pairs, 2, 2, top, depth),
                tiles,
            )
        )
    )


def solution(mesh):
    placed = (
        P("occ", "virt"),
        P(("occ", "virt"), None, None),
        P(("occ", "virt")),
        P(("occ", "virt")),
        P("virt"),
        P("occ"),
    )
    return jax.shard_map(
        functools.partial(body, mesh.shape["occ"], mesh.shape["virt"]),
        mesh=mesh, in_specs=placed, out_specs=P("virt", "occ"), check_vma=False,
    )
```

```python
import functools

import jax
import jax.numpy as jnp
from jax import lax
from jax.experimental import pallas as pl
from jax.experimental.pallas import tpu as pltpu
from jax.sharding import PartitionSpec as P

MESH = pl.DeviceIdType.MESH
TAIL = 1
LAG = 2
CHUNKS = 4
REACHES = (2, 2)
GRANT = 50 * 2**20


def flip(index, mask, size):
    out = index * 0
    bit = 1
    while bit < size:
        digit = lax.rem(lax.div(index, bit), 2)
        if mask & bit:
            digit = 1 - digit
        out = out + digit * bit
        bit *= 2
    return out


def kernel(
    no, nv, reaches,
    code_in, count_in, occ_in, virt_in, amp_in, tiles_in, out_ref,
    code, count, occ_energy, virt_energy, slot_map, slot_of,
    tiles, high, low, amps, lhss, parts, partner_parts, summeds, arriveds, own_tail, stage, gap,
    small_sem, slot_sem, tile_sem, own_sem, next_in, plane_in,
    gather_send, gather_recv, core_send, core_recv, chip_send, chip_recv,
):
    o = lax.axis_index("occ")
    v = lax.axis_index("virt")
    core = lax.rem(v, 2)
    chip = lax.div(v, 2)
    chips = nv // 2
    depth = amp_in.shape[-1]
    tile = tiles_in.shape[1]
    dest, width = out_ref.shape
    pairs = amp_in.shape[0]
    reach = max(reaches)
    phases = len(amps)
    levels = [summed.shape[1] for summed in summeds]
    starts = [sum(levels[:phase]) for phase in range(phases)]
    col_tiles = width // tile
    positions = (depth // tile) * col_tiles
    slots = tiles_in.shape[0]
    other_core = (o, v + 1 - 2 * core)

    small = [
        pltpu.make_async_copy(source, target, small_sem.at[number])
        for number, (source, target) in enumerate(
            ((code_in, code), (count_in, count), (occ_in, occ_energy), (virt_in, virt_energy))
        )
    ]
    own_copies = [
        pltpu.make_async_copy(amp_in.at[:, :, 1], own_tail, own_sem.at[1]),
        pltpu.make_async_copy(amp_in.at[:, :, 0], amps[0].at[o], own_sem.at[0]),
    ]
    tile_copy = pltpu.make_async_copy(tiles_in, tiles.at[pl.ds(0, slots)], tile_sem)

    barrier = pltpu.get_barrier_semaphore()

    def meet(device):
        pl.semaphore_signal(barrier, inc=1, device_id=device, device_id_type=MESH)

    for hop in range(1, reach + 1):

        @pl.when(o + hop < no)
        def _():
            meet((o + hop, v))

    def one(condition):
        return condition.astype(jnp.int32)

    before = one(core == 1)
    after = one(core == 0)
    for mask in range(1, chips):
        there = flip(chip, mask, chips)
        before = before + one(there < chip)
        after = after + one(there > chip)

        @pl.when(there > chip)
        def _():
            meet((o, 2 * there + core))

    @pl.when(core == 0)
    def _():
        meet(other_core)

    own_copies[0].start()
    for copy in small:
        copy.start()
    own_copies[1].start()
    tile_copy.start()

    for hop in range(1, reach + 1):
        before = before + one(o >= hop)

    @pl.when(before > 0)
    def _():
        pl.semaphore_wait(barrier, before)

    for hop in range(1, reach + 1):

        @pl.when(o >= hop)
        def _():
            pl.semaphore_signal(
                next_in.at[hop - 1], inc=1, device_id=(o - hop, v), device_id_type=MESH
            )

    def gather_copy(which, phase, hop, side, source=None):
        held = amps[phase].at[which]
        return pltpu.make_async_remote_copy(
            src_ref=held if source is None else source,
            dst_ref=held,
            send_sem=gather_send.at[side, which, hop - 1, phase],
            recv_sem=gather_recv.at[which, phase],
            device_id=(o + hop * (2 * side - 1), v),
            device_id_type=MESH,
        )

    def exists(hop, side):
        return o + hop < no if side else o >= hop

    def send_own(phase, hop, side):
        @pl.when(exists(hop, side))
        def _():
            gather_copy(o, phase, hop, side, amp_in.at[:, :, 0] if phase == 0 else None).start()

    def send_all(phase, side):
        for hop in range(reaches[phase], 0, -1):
            send_own(phase, hop, side)

    send_all(0, 0)

    for mask in range(1, chips):
        there = flip(chip, mask, chips)

        @pl.when(there < chip)
        def _():
            pl.semaphore_signal(
                plane_in, inc=1, device_id=(o, 2 * there + core), device_id_type=MESH
            )

    @pl.when(core == 1)
    def _():
        pl.semaphore_signal(plane_in, inc=1, device_id=other_core, device_id_type=MESH)

    own_copies[0].wait()
    for phase in range(1, phases):
        level = levels[phase]
        for pair in range(pairs):
            for side in range(2):
                amps[phase][o, pair, pl.ds(side * level, level)] = own_tail[
                    pair, side, pl.ds((phase - 1) * level, level)
                ]
    for phase in range(1, phases):
        send_all(phase, 0)

    tiles[slots] = jnp.zeros(tiles.shape[1:], tiles.dtype)
    small[0].wait()
    small[1].wait()
    lanes = slot_map.shape[1]
    place_index = lax.broadcasted_iota(jnp.int32, slot_map.shape, 0) * lanes + (
        lax.broadcasted_iota(jnp.int32, slot_map.shape, 1)
    )
    found = jnp.full(slot_map.shape, slots, jnp.int32)
    live = count[0]
    for slot in range(slots):
        found = jnp.where(place_index == jnp.where(slot < live, code[slot], -1), slot, found)
    slot_map[...] = found
    slot_copy = pltpu.make_async_copy(slot_map, slot_of, slot_sem)
    slot_copy.start()

    def place(position, carry):
        value = tiles[slot_of[lax.div(position, lanes), lax.rem(position, lanes)]]
        rounded = value.astype(jnp.bfloat16)
        at_row = pl.multiple_of(lax.div(position, col_tiles) * tile, tile)
        at_col = pl.multiple_of(lax.rem(position, col_tiles) * tile, tile)
        high[pl.ds(at_row, tile), pl.ds(at_col, tile)] = rounded
        low[pl.ds(at_row, tile), pl.ds(at_col, tile)] = (
            value - rounded.astype(jnp.float32)
        ).astype(jnp.bfloat16)
        return carry

    tile_copy.wait()
    slot_copy.wait()
    for hop in range(1, reach + 1):

        @pl.when(exists(hop, 1))
        def _():
            pl.semaphore_wait(next_in.at[hop - 1], 1)

        if hop <= reaches[0]:
            send_own(0, hop, 1)
        lax.fori_loop(
            positions * (hop - 1) // reach, positions * hop // reach, place, 0
        )
    own_copies[1].wait()
    small[2].wait()
    small[3].wait()
    row_index = lax.broadcasted_iota(jnp.int32, gap.shape, 0)
    energy = jnp.zeros(gap.shape, jnp.float32)
    for row in range(dest):
        energy = jnp.where(row_index == row, occ_energy[row], energy)
    gap[...] = virt_energy[...] - energy

    def relay(phase, distance, sides=(0, 1)):
        for side in sides:

            @pl.when(exists(distance, 1 - side) & exists(1, side))
            def _():
                which = o + distance * (1 - 2 * side)
                gather_copy(which, phase, 1, side).wait_recv()
                for hop in range(reaches[phase], 0, -1):

                    @pl.when(exists(hop, side))
                    def _():
                        gather_copy(which, phase, hop, side).start()

    def arrive(phase, distance):
        for side in range(2):
            here = exists(distance, 1 - side)
            if distance % reaches[phase] == 0 and distance < no - 1:
                here = here & jnp.logical_not(exists(1, side))

            @pl.when(here)
            def _():
                gather_copy(o + distance * (1 - 2 * side), phase, 1, side).wait_recv()

    def relays(wanted, sides):
        for distance in range(1, no - 1):
            for phase in wanted:
                if distance % reaches[phase] == 0:
                    relay(phase, distance, sides)

    relays([0], [1])
    for phase in range(1, phases):
        send_all(phase, 1)

    chunk = width // CHUNKS

    def split(phase):
        rows = lhss[phase].shape[0] // 2
        half = rows // 2
        level = levels[phase]
        if phase:
            for which in range(no):
                for pair in range(pairs):
                    for side in range(2):
                        stage[pl.ds(side * half + (which * pairs + pair) * level, level)] = amps[
                            phase
                        ][which, pair, pl.ds(side * level, level)]
        for side in range(2):
            if phase:
                value = stage[pl.ds(side * half, half)]
            else:
                value = amps[0][:, :, side].reshape(half, depth)
            rounded = value.astype(jnp.bfloat16)
            lhss[phase][pl.ds(side * half, half)] = rounded
            lhss[phase][pl.ds(rows + side * half, half)] = (
                value - rounded.astype(jnp.float32)
            ).astype(jnp.bfloat16)

    def core_copy(phase, at):
        cols = pl.ds(at * chunk, chunk)
        return pltpu.make_async_remote_copy(
            src_ref=parts[phase].at[1 - core, :, cols],
            dst_ref=partner_parts[phase].at[:, cols],
            send_sem=core_send.at[phase],
            recv_sem=core_recv.at[phase, at],
            device_id=other_core,
            device_id_type=MESH,
        )

    def chip_copy(phase, mask, at):
        cols = pl.ds(at * chunk, chunk)
        there = flip(chip, mask, chips)
        return pltpu.make_async_remote_copy(
            src_ref=summeds[phase].at[there, :, cols],
            dst_ref=arriveds[phase].at[mask - 1, :, cols],
            send_sem=chip_send.at[phase],
            recv_sem=chip_recv.at[phase],
            device_id=(o, 2 * there + core),
            device_id_type=MESH,
        )

    def every_core_copy(phase):
        return pltpu.make_async_remote_copy(
            src_ref=parts[phase].at[1 - core],
            dst_ref=partner_parts[phase],
            send_sem=core_send.at[phase],
            recv_sem=core_recv.at[phase, 0],
            device_id=other_core,
            device_id_type=MESH,
        )

    def every_chip_copy(phase):
        return pltpu.make_async_remote_copy(
            src_ref=summeds[phase].at[pl.ds(0, chips - 1)],
            dst_ref=arriveds[phase],
            send_sem=chip_send.at[phase],
            recv_sem=chip_recv.at[phase],
            device_id=other_core,
            device_id_type=MESH,
        )

    def multiply(phase, at):
        rows = lhss[phase].shape[0] // 2
        cols = pl.ds(at * chunk, chunk)
        wide = jnp.dot(lhss[phase][...], high[:, cols], preferred_element_type=jnp.float32)
        narrow = jnp.dot(
            lhss[phase][pl.ds(0, rows)], low[:, cols], preferred_element_type=jnp.float32
        )
        total = wide[:rows] + (wide[rows:] + narrow)
        parts[phase][:, :, cols] = total.reshape(2, rows // 2, chunk)
        core_copy(phase, at).start()

    def pass_on(phase, at):
        level = levels[phase]
        cols = pl.ds(at * chunk, chunk)
        core_copy(phase, at).wait_recv()
        for there in range(chips):
            rows = pl.ds(there * level, level)
            summeds[phase][there, :, cols] = (
                parts[phase][core, rows, cols] + partner_parts[phase][rows, cols]
            )
        for mask in range(chips - 1, 0, -1):
            chip_copy(phase, mask, at).start()

    relays([0], [0])
    relays(range(1, phases), [0, 1])
    for phase in range(phases):
        for distance in range(1, no):
            arrive(phase, distance)
        split(phase)
        if phase == 0:

            @pl.when(after > 0)
            def _():
                pl.semaphore_wait(plane_in, after)

        passed = 0
        for at in range(CHUNKS):
            multiply(phase, at)
            if at >= LAG:
                pass_on(phase, passed)
                passed += 1
        for at in range(passed, CHUNKS):
            pass_on(phase, at)

    for phase in range(phases):
        for side in range(2):
            for distance in range(0, no, reaches[phase]):

                @pl.when(exists(distance, 1 - side))
                def _():
                    which = o + distance * (1 - 2 * side)
                    for hop in range(1, reaches[phase] + 1):

                        @pl.when(exists(hop, side))
                        def _():
                            gather_copy(which, phase, hop, side).wait_send()

    for phase in range(phases):
        rows = pl.ds(starts[phase], levels[phase])
        every_core_copy(phase).wait_send()
        every_chip_copy(phase).wait_recv()
        total = summeds[phase][chip]
        for mask in range(1, chips):
            total = total + arriveds[phase][mask - 1]
        out_ref[rows] = total / gap[rows]
        every_chip_copy(phase).wait_send()


def body(no, nv, amplitudes, tiles, tile_code, tile_count, occ_energy, virt_energy):
    block, depth = amplitudes.shape
    slots, tile, _ = tiles.shape
    width = virt_energy.shape[0]
    dest = occ_energy.shape[0]
    chips = nv // 2
    top = dest // 2
    levels = [top] + [(dest - top) // TAIL] * TAIL
    phases = len(levels)
    pairs = block // (2 * dest)
    reaches = REACHES if no <= 4 else (1,) * phases
    reach = max(reaches)
    map_shape = (max(8, (depth // tile) * (width // tile) // 128), 128)
    f32, bf16, i32 = jnp.float32, jnp.bfloat16, jnp.int32
    vmem, smem, dma = pltpu.VMEM, pltpu.SMEM, pltpu.SemaphoreType.DMA
    regular = pltpu.SemaphoreType.REGULAR
    return pl.pallas_call(
        functools.partial(kernel, no, nv, reaches),
        out_shape=jax.ShapeDtypeStruct((dest, width), f32),
        in_specs=[pl.BlockSpec(memory_space=pltpu.HBM)] * 6,
        out_specs=pl.BlockSpec(memory_space=pltpu.VMEM),
        scratch_shapes=[
            smem(tile_code.shape, i32),
            smem(tile_count.shape, i32),
            smem((dest,), f32),
            vmem((1, width), f32),
            vmem(map_shape, i32),
            smem(map_shape, i32),
            vmem((slots + 1, tile, tile), f32),
            vmem((depth, width), bf16),
            vmem((depth, width), bf16),
            [vmem((no, pairs, 2, top, depth), f32)]
            + [vmem((no, pairs, 2 * level, depth), f32) for level in levels[1:]],
            [vmem((4 * chips * level, depth), bf16) for level in levels],
            [vmem((2, chips * level, width), f32) for level in levels],
            [vmem((chips * level, width), f32) for level in levels],
            [vmem((chips, level, width), f32) for level in levels],
            [vmem((chips - 1, level, width), f32) for level in levels],
            vmem((pairs, 2, dest - top, depth), f32),
            vmem((2 * chips * levels[-1], depth), f32),
            vmem((dest, width), f32),
            dma((4,)),
            dma,
            dma,
            dma((2,)),
            regular((reach,)),
            regular,
            dma((2, no, reach, phases)),
            dma((no, phases)),
            dma((phases,)),
            dma((phases, CHUNKS)),
            dma((phases,)),
            dma((phases,)),
        ],
        compiler_params=pltpu.CompilerParams(
            collective_id=0, has_side_effects=True, vmem_limit_bytes=GRANT
        ),
    )(
        *(
            a if a is tile_count else pltpu.with_memory_space_constraint(a, pltpu.HBM)
            for a in (
                tile_code,
                tile_count,
                occ_energy,
                virt_energy.reshape(1, width),
                amplitudes.reshape(pairs, 2, 2, top, depth),
                tiles,
            )
        )
    )


def solution(mesh):
    placed = (
        P("occ", "virt"),
        P(("occ", "virt"), None, None),
        P(("occ", "virt")),
        P(("occ", "virt")),
        P("virt"),
        P("occ"),
    )
    return jax.shard_map(
        functools.partial(body, mesh.shape["occ"], mesh.shape["virt"]),
        mesh=mesh, in_specs=placed, out_specs=P("virt", "occ"), check_vma=False,
    )
```

```python
import functools

import jax
import jax.numpy as jnp
from jax import lax
from jax.experimental import pallas as pl
from jax.experimental.pallas import tpu as pltpu
from jax.sharding import PartitionSpec as P

MESH = pl.DeviceIdType.MESH
TAIL = 1
DEFER = (0, 0)
LAG = 2
EARLY = 0
KEEP = 1
CHUNKS = 4
REACHES = ((2, 2), (3, 2))
GRANT = 50 * 2**20


def flip(index, mask, size):
    out = index * 0
    bit = 1
    while bit < size:
        digit = lax.rem(lax.div(index, bit), 2)
        if mask & bit:
            digit = 1 - digit
        out = out + digit * bit
        bit *= 2
    return out


def kernel(
    no, nv, reaches, deferred,
    code_in, count_in, occ_in, virt_in, amp_in, tiles_in, out_ref,
    code, count, occ_energy, virt_energy, slot_map, slot_of,
    tiles, high, low, amps, lhss, parts, partner_parts, summeds, arriveds, own_tail, stage, gap,
    small_sem, slot_sem, tile_sem, own_sem, next_in, plane_in,
    gather_send, gather_recv, core_send, core_recv, chip_send, chip_recv,
):
    o = lax.axis_index("occ")
    v = lax.axis_index("virt")
    core = lax.rem(v, 2)
    chip = lax.div(v, 2)
    chips = nv // 2
    depth = amp_in.shape[-1]
    tile = tiles_in.shape[1]
    dest, width = out_ref.shape
    pairs = amp_in.shape[0]
    reach = max(max(side) for side in reaches)
    phases = len(amps)
    levels = [summed.shape[1] for summed in summeds]
    starts = [sum(levels[:phase]) for phase in range(phases)]
    col_tiles = width // tile
    positions = (depth // tile) * col_tiles
    slots = tiles_in.shape[0]
    other_core = (o, v + 1 - 2 * core)

    small = [
        pltpu.make_async_copy(source, target, small_sem.at[number])
        for number, (source, target) in enumerate(
            ((code_in, code), (count_in, count), (occ_in, occ_energy), (virt_in, virt_energy))
        )
    ]
    own_copies = [
        pltpu.make_async_copy(amp_in.at[:, :, 1], own_tail, own_sem.at[1]),
        pltpu.make_async_copy(amp_in.at[:, :, 0], amps[0].at[o], own_sem.at[0]),
    ]
    tile_copy = pltpu.make_async_copy(tiles_in, tiles.at[pl.ds(0, slots)], tile_sem)

    barrier = pltpu.get_barrier_semaphore()

    def meet(device):
        pl.semaphore_signal(barrier, inc=1, device_id=device, device_id_type=MESH)

    for hop in range(1, reach + 1):

        @pl.when(o + hop < no)
        def _():
            meet((o + hop, v))

    def one(condition):
        return condition.astype(jnp.int32)

    before = one(core == 1)
    after = one(core == 0)
    for mask in range(1, chips):
        there = flip(chip, mask, chips)
        before = before + one(there < chip)
        after = after + one(there > chip)

        @pl.when(there > chip)
        def _():
            meet((o, 2 * there + core))

    @pl.when(core == 0)
    def _():
        meet(other_core)

    own_copies[0].start()
    for copy in small:
        copy.start()
    own_copies[1].start()
    tile_copy.start()

    for hop in range(1, reach + 1):
        before = before + one(o >= hop)

    @pl.when(before > 0)
    def _():
        pl.semaphore_wait(barrier, before)

    for hop in range(1, reach + 1):

        @pl.when(o >= hop)
        def _():
            pl.semaphore_signal(
                next_in.at[hop - 1], inc=1, device_id=(o - hop, v), device_id_type=MESH
            )

    def gather_copy(which, phase, hop, side, source=None):
        held = amps[phase].at[which]
        return pltpu.make_async_remote_copy(
            src_ref=held if source is None else source,
            dst_ref=held,
            send_sem=gather_send.at[side, which, hop - 1, phase],
            recv_sem=gather_recv.at[which, phase],
            device_id=(o + hop * (2 * side - 1), v),
            device_id_type=MESH,
        )

    def exists(hop, side):
        return o + hop < no if side else o >= hop

    def send_own(phase, hop, side, wanted=True):
        @pl.when(exists(hop, side) & wanted)
        def _():
            gather_copy(o, phase, hop, side, amp_in.at[:, :, 0] if phase == 0 else None).start()

    def send_first(phase, side):
        for hop in range(reaches[side][phase], 0, -1):
            if hop == 1 and deferred[side]:
                send_own(phase, 1, side, jnp.logical_not(exists(2, side)))
            else:
                send_own(phase, hop, side)

    def send_rest(phase, side):
        if deferred[side]:
            send_own(phase, 1, side, exists(2, side))

    send_first(0, 0)

    for mask in range(1, chips):
        there = flip(chip, mask, chips)

        @pl.when(there < chip)
        def _():
            pl.semaphore_signal(
                plane_in, inc=1, device_id=(o, 2 * there + core), device_id_type=MESH
            )

    @pl.when(core == 1)
    def _():
        pl.semaphore_signal(plane_in, inc=1, device_id=other_core, device_id_type=MESH)

    own_copies[0].wait()
    for phase in range(1, phases):
        level = levels[phase]
        for pair in range(pairs):
            for side in range(2):
                amps[phase][o, pair, pl.ds(side * level, level)] = own_tail[
                    pair, side, pl.ds((phase - 1) * level, level)
                ]
    for phase in range(1, phases):
        send_first(phase, 0)

    tiles[slots] = jnp.zeros(tiles.shape[1:], tiles.dtype)
    small[0].wait()
    small[1].wait()
    lanes = slot_map.shape[1]
    place_index = lax.broadcasted_iota(jnp.int32, slot_map.shape, 0) * lanes + (
        lax.broadcasted_iota(jnp.int32, slot_map.shape, 1)
    )
    found = jnp.full(slot_map.shape, slots, jnp.int32)
    live = count[0]
    for slot in range(slots):
        found = jnp.where(place_index == jnp.where(slot < live, code[slot], -1), slot, found)
    slot_map[...] = found
    slot_copy = pltpu.make_async_copy(slot_map, slot_of, slot_sem)
    slot_copy.start()

    def place(position, carry):
        value = tiles[slot_of[lax.div(position, lanes), lax.rem(position, lanes)]]
        rounded = value.astype(jnp.bfloat16)
        at_row = pl.multiple_of(lax.div(position, col_tiles) * tile, tile)
        at_col = pl.multiple_of(lax.rem(position, col_tiles) * tile, tile)
        high[pl.ds(at_row, tile), pl.ds(at_col, tile)] = rounded
        low[pl.ds(at_row, tile), pl.ds(at_col, tile)] = (
            value - rounded.astype(jnp.float32)
        ).astype(jnp.bfloat16)
        return carry

    tile_copy.wait()
    slot_copy.wait()
    for hop in range(1, reach + 1):

        @pl.when(exists(hop, 1))
        def _():
            pl.semaphore_wait(next_in.at[hop - 1], 1)

        if hop == 1 and deferred[1]:
            send_own(0, 1, 1, jnp.logical_not(exists(2, 1)))
        elif hop <= reaches[1][0]:
            send_own(0, hop, 1)
        lax.fori_loop(
            positions * (hop - 1) // reach, positions * hop // reach, place, 0
        )
    own_copies[1].wait()
    small[2].wait()
    small[3].wait()
    row_index = lax.broadcasted_iota(jnp.int32, gap.shape, 0)
    energy = jnp.zeros(gap.shape, jnp.float32)
    for row in range(dest):
        energy = jnp.where(row_index == row, occ_energy[row], energy)
    gap[...] = virt_energy[...] - energy

    def relay(phase, distance, side):
        @pl.when(exists(distance, 1 - side) & exists(1, side))
        def _():
            which = o + distance * (1 - 2 * side)
            gather_copy(which, phase, 1, side).wait_recv()
            for hop in range(reaches[side][phase], 0, -1):

                @pl.when(exists(hop, side))
                def _():
                    gather_copy(which, phase, hop, side).start()

    def arrive(phase, distance):
        for side in range(2):
            here = exists(distance, 1 - side)
            if distance % reaches[side][phase] == 0 and distance < no - 1:
                here = here & jnp.logical_not(exists(1, side))

            @pl.when(here)
            def _():
                gather_copy(o + distance * (1 - 2 * side), phase, 1, side).wait_recv()

    def relays(wanted, sides):
        for distance in range(1, no - 1):
            for phase in wanted:
                for side in sides:
                    if distance % reaches[side][phase] == 0:
                        relay(phase, distance, side)

    relays([0], [1])
    for phase in range(1, phases):
        send_first(phase, 1)
    for phase in range(phases):
        for side in range(2):
            send_rest(phase, side)

    chunk = width // CHUNKS

    def split(phase):
        rows = lhss[phase].shape[0] // 2
        half = rows // 2
        level = levels[phase]
        if phase:
            for which in range(no):
                for pair in range(pairs):
                    for side in range(2):
                        stage[pl.ds(side * half + (which * pairs + pair) * level, level)] = amps[
                            phase
                        ][which, pair, pl.ds(side * level, level)]
        for side in range(2):
            if phase:
                value = stage[pl.ds(side * half, half)]
            else:
                value = amps[0][:, :, side].reshape(half, depth)
            rounded = value.astype(jnp.bfloat16)
            lhss[phase][pl.ds(side * half, half)] = rounded
            lhss[phase][pl.ds(rows + side * half, half)] = (
                value - rounded.astype(jnp.float32)
            ).astype(jnp.bfloat16)

    def core_copy(phase, at):
        cols = pl.ds(at * chunk, chunk)
        return pltpu.make_async_remote_copy(
            src_ref=parts[phase].at[1 - core, :, cols],
            dst_ref=partner_parts[phase].at[:, cols],
            send_sem=core_send.at[phase],
            recv_sem=core_recv.at[phase, at],
            device_id=other_core,
            device_id_type=MESH,
        )

    def chip_copy(phase, mask, at):
        cols = pl.ds(at * chunk, chunk)
        there = flip(chip, mask, chips)
        return pltpu.make_async_remote_copy(
            src_ref=summeds[phase].at[there, :, cols],
            dst_ref=arriveds[phase].at[mask - 1, :, cols],
            send_sem=chip_send.at[phase],
            recv_sem=chip_recv.at[phase],
            device_id=(o, 2 * there + core),
            device_id_type=MESH,
        )

    def every_core_copy(phase):
        return pltpu.make_async_remote_copy(
            src_ref=parts[phase].at[1 - core],
            dst_ref=partner_parts[phase],
            send_sem=core_send.at[phase],
            recv_sem=core_recv.at[phase, 0],
            device_id=other_core,
            device_id_type=MESH,
        )

    def every_chip_copy(phase):
        return pltpu.make_async_remote_copy(
            src_ref=summeds[phase].at[pl.ds(0, chips - 1)],
            dst_ref=arriveds[phase],
            send_sem=chip_send.at[phase],
            recv_sem=chip_recv.at[phase],
            device_id=other_core,
            device_id_type=MESH,
        )

    def multiply(phase, at):
        rows = lhss[phase].shape[0] // 2
        cols = pl.ds(at * chunk, chunk)
        wide = jnp.dot(lhss[phase][...], high[:, cols], preferred_element_type=jnp.float32)
        narrow = jnp.dot(
            lhss[phase][pl.ds(0, rows)], low[:, cols], preferred_element_type=jnp.float32
        )
        total = wide[:rows] + (wide[rows:] + narrow)
        parts[phase][:, :, cols] = total.reshape(2, rows // 2, chunk)
        core_copy(phase, at).start()

    def pass_on(phase, at):
        level = levels[phase]
        cols = pl.ds(at * chunk, chunk)
        core_copy(phase, at).wait_recv()
        for there in range(chips):
            rows = pl.ds(there * level, level)
            summeds[phase][there, :, cols] = (
                parts[phase][core, rows, cols] + partner_parts[phase][rows, cols]
            )
        for mask in range(chips - 1, 0, -1):
            chip_copy(phase, mask, at).start()

    relays([0], [0])
    relays(range(1, phases), [0, 1])
    for phase in range(phases):
        for distance in range(1, no):
            arrive(phase, distance)
        split(phase)
        if phase == 0:

            @pl.when(after > 0)
            def _():
                pl.semaphore_wait(plane_in, after)

        kept = KEEP if phase < phases - 1 else 0
        late = LAG if phase < phases - 1 else EARLY
        for at in range(CHUNKS + LAG):
            if at < CHUNKS:
                multiply(phase, at)
                if phase and at < KEEP:
                    pass_on(phase - 1, CHUNKS - KEEP + at)
            if late == LAG:
                if LAG <= at < CHUNKS + LAG - kept:
                    pass_on(phase, at - LAG)
            else:
                for which, lag in enumerate((late, LAG)):
                    if lag <= at < CHUNKS + lag - kept:

                        @pl.when(core == which)
                        def _():
                            pass_on(phase, at - lag)

    for phase in range(phases):
        for side in range(2):
            for distance in range(0, no, reaches[side][phase]):

                @pl.when(exists(distance, 1 - side))
                def _():
                    which = o + distance * (1 - 2 * side)
                    for hop in range(1, reaches[side][phase] + 1):

                        @pl.when(exists(hop, side))
                        def _():
                            gather_copy(which, phase, hop, side).wait_send()

    for phase in range(phases):
        rows = pl.ds(starts[phase], levels[phase])
        every_core_copy(phase).wait_send()
        every_chip_copy(phase).wait_recv()
        total = summeds[phase][chip]
        for mask in range(1, chips):
            total = total + arriveds[phase][mask - 1]
        out_ref[rows] = total / gap[rows]
        every_chip_copy(phase).wait_send()


def body(no, nv, amplitudes, tiles, tile_code, tile_count, occ_energy, virt_energy):
    block, depth = amplitudes.shape
    slots, tile, _ = tiles.shape
    width = virt_energy.shape[0]
    dest = occ_energy.shape[0]
    chips = nv // 2
    top = dest // 2
    levels = [top] + [(dest - top) // TAIL] * TAIL
    phases = len(levels)
    pairs = block // (2 * dest)
    close = no <= 4
    reaches = REACHES if close else ((1,) * phases,) * 2
    deferred = DEFER if close else (0, 0)
    reach = max(max(side) for side in reaches)
    map_shape = (max(8, (depth // tile) * (width // tile) // 128), 128)
    f32, bf16, i32 = jnp.float32, jnp.bfloat16, jnp.int32
    vmem, smem, dma = pltpu.VMEM, pltpu.SMEM, pltpu.SemaphoreType.DMA
    regular = pltpu.SemaphoreType.REGULAR
    return pl.pallas_call(
        functools.partial(kernel, no, nv, reaches, deferred),
        out_shape=jax.ShapeDtypeStruct((dest, width), f32),
        in_specs=[pl.BlockSpec(memory_space=pltpu.HBM)] * 6,
        out_specs=pl.BlockSpec(memory_space=pltpu.VMEM),
        scratch_shapes=[
            smem(tile_code.shape, i32),
            smem(tile_count.shape, i32),
            smem((dest,), f32),
            vmem((1, width), f32),
            vmem(map_shape, i32),
            smem(map_shape, i32),
            vmem((slots + 1, tile, tile), f32),
            vmem((depth, width), bf16),
            vmem((depth, width), bf16),
            [vmem((no, pairs, 2, top, depth), f32)]
            + [vmem((no, pairs, 2 * level, depth), f32) for level in levels[1:]],
            [vmem((4 * chips * level, depth), bf16) for level in levels],
            [vmem((2, chips * level, width), f32) for level in levels],
            [vmem((chips * level, width), f32) for level in levels],
            [vmem((chips, level, width), f32) for level in levels],
            [vmem((chips - 1, level, width), f32) for level in levels],
            vmem((pairs, 2, dest - top, depth), f32),
            vmem((2 * chips * levels[-1], depth), f32),
            vmem((dest, width), f32),
            dma((4,)),
            dma,
            dma,
            dma((2,)),
            regular((reach,)),
            regular,
            dma((2, no, reach, phases)),
            dma((no, phases)),
            dma((phases,)),
            dma((phases, CHUNKS)),
            dma((phases,)),
            dma((phases,)),
        ],
        compiler_params=pltpu.CompilerParams(
            collective_id=0, has_side_effects=True, vmem_limit_bytes=GRANT
        ),
    )(
        *(
            a if a is tile_count else pltpu.with_memory_space_constraint(a, pltpu.HBM)
            for a in (
                tile_code,
                tile_count,
                occ_energy,
                virt_energy.reshape(1, width),
                amplitudes.reshape(pairs, 2, 2, top, depth),
                tiles,
            )
        )
    )


def solution(mesh):
    placed = (
        P("occ", "virt"),
        P(("occ", "virt"), None, None),
        P(("occ", "virt")),
        P(("occ", "virt")),
        P("virt"),
        P("occ"),
    )
    return jax.shard_map(
        functools.partial(body, mesh.shape["occ"], mesh.shape["virt"]),
        mesh=mesh, in_specs=placed, out_specs=P("virt", "occ"), check_vma=False,
    )
```

```python
import functools

import jax
import jax.numpy as jnp
from jax import lax
from jax.experimental import pallas as pl
from jax.experimental.pallas import tpu as pltpu
from jax.sharding import PartitionSpec as P

MESH = pl.DeviceIdType.MESH
TAIL = 1
DEFER = (0, 2)
LAG = 2
EARLY = 0
KEEP = 1
CHUNKS = 4
REACHES = ((2, 2), (3, 2))
GRANT = 50 * 2**20


def flip(index, mask, size):
    out = index * 0
    bit = 1
    while bit < size:
        digit = lax.rem(lax.div(index, bit), 2)
        if mask & bit:
            digit = 1 - digit
        out = out + digit * bit
        bit *= 2
    return out


def kernel(
    no, nv, reaches, deferred,
    code_in, count_in, occ_in, virt_in, amp_in, tiles_in, out_ref,
    code, count, occ_energy, virt_energy, slot_map, slot_of,
    tiles, high, low, amps, lhss, parts, partner_parts, summeds, arriveds, own_tail, stage, gap,
    small_sem, slot_sem, tile_sem, own_sem, next_in, plane_in,
    gather_send, gather_recv, core_send, core_recv, chip_send, chip_recv,
):
    o = lax.axis_index("occ")
    v = lax.axis_index("virt")
    core = lax.rem(v, 2)
    chip = lax.div(v, 2)
    chips = nv // 2
    depth = amp_in.shape[-1]
    tile = tiles_in.shape[1]
    dest, width = out_ref.shape
    pairs = amp_in.shape[0]
    reach = max(max(side) for side in reaches)
    phases = len(amps)
    levels = [summed.shape[1] for summed in summeds]
    starts = [sum(levels[:phase]) for phase in range(phases)]
    col_tiles = width // tile
    positions = (depth // tile) * col_tiles
    slots = tiles_in.shape[0]
    other_core = (o, v + 1 - 2 * core)

    small = [
        pltpu.make_async_copy(source, target, small_sem.at[number])
        for number, (source, target) in enumerate(
            ((code_in, code), (count_in, count), (occ_in, occ_energy), (virt_in, virt_energy))
        )
    ]
    own_copies = [
        pltpu.make_async_copy(amp_in.at[:, :, 1], own_tail, own_sem.at[1]),
        pltpu.make_async_copy(amp_in.at[:, :, 0], amps[0].at[o], own_sem.at[0]),
    ]
    tile_copy = pltpu.make_async_copy(tiles_in, tiles.at[pl.ds(0, slots)], tile_sem)

    barrier = pltpu.get_barrier_semaphore()

    def meet(device):
        pl.semaphore_signal(barrier, inc=1, device_id=device, device_id_type=MESH)

    for hop in range(1, reach + 1):

        @pl.when(o + hop < no)
        def _():
            meet((o + hop, v))

    def one(condition):
        return condition.astype(jnp.int32)

    before = one(core == 1)
    after = one(core == 0)
    for mask in range(1, chips):
        there = flip(chip, mask, chips)
        before = before + one(there < chip)
        after = after + one(there > chip)

        @pl.when(there > chip)
        def _():
            meet((o, 2 * there + core))

    @pl.when(core == 0)
    def _():
        meet(other_core)

    own_copies[0].start()
    for copy in small:
        copy.start()
    own_copies[1].start()
    tile_copy.start()

    for hop in range(1, reach + 1):
        before = before + one(o >= hop)

    @pl.when(before > 0)
    def _():
        pl.semaphore_wait(barrier, before)

    for hop in range(1, reach + 1):

        @pl.when(o >= hop)
        def _():
            pl.semaphore_signal(
                next_in.at[hop - 1], inc=1, device_id=(o - hop, v), device_id_type=MESH
            )

    def gather_copy(which, phase, hop, side, source=None):
        held = amps[phase].at[which]
        return pltpu.make_async_remote_copy(
            src_ref=held if source is None else source,
            dst_ref=held,
            send_sem=gather_send.at[side, which, hop - 1, phase],
            recv_sem=gather_recv.at[which, phase],
            device_id=(o + hop * (2 * side - 1), v),
            device_id_type=MESH,
        )

    def exists(hop, side):
        return o + hop < no if side else o >= hop

    def send_own(phase, hop, side, wanted=True):
        @pl.when(exists(hop, side) & wanted)
        def _():
            gather_copy(o, phase, hop, side, amp_in.at[:, :, 0] if phase == 0 else None).start()

    def send_first(phase, side):
        for hop in range(reaches[side][phase], 0, -1):
            if hop == 1 and deferred[side] and phase >= deferred[side] - 1:
                send_own(phase, 1, side, jnp.logical_not(exists(2, side)))
            else:
                send_own(phase, hop, side)

    def send_rest(phase, side):
        if deferred[side] and phase >= deferred[side] - 1:
            send_own(phase, 1, side, exists(2, side))

    send_first(0, 0)

    for mask in range(1, chips):
        there = flip(chip, mask, chips)

        @pl.when(there < chip)
        def _():
            pl.semaphore_signal(
                plane_in, inc=1, device_id=(o, 2 * there + core), device_id_type=MESH
            )

    @pl.when(core == 1)
    def _():
        pl.semaphore_signal(plane_in, inc=1, device_id=other_core, device_id_type=MESH)

    own_copies[0].wait()
    for phase in range(1, phases):
        level = levels[phase]
        for pair in range(pairs):
            for side in range(2):
                amps[phase][o, pair, pl.ds(side * level, level)] = own_tail[
                    pair, side, pl.ds((phase - 1) * level, level)
                ]
    for phase in range(1, phases):
        send_first(phase, 0)

    tiles[slots] = jnp.zeros(tiles.shape[1:], tiles.dtype)
    small[0].wait()
    small[1].wait()
    lanes = slot_map.shape[1]
    place_index = lax.broadcasted_iota(jnp.int32, slot_map.shape, 0) * lanes + (
        lax.broadcasted_iota(jnp.int32, slot_map.shape, 1)
    )
    found = jnp.full(slot_map.shape, slots, jnp.int32)
    live = count[0]
    for slot in range(slots):
        found = jnp.where(place_index == jnp.where(slot < live, code[slot], -1), slot, found)
    slot_map[...] = found
    slot_copy = pltpu.make_async_copy(slot_map, slot_of, slot_sem)
    slot_copy.start()

    def place(position, carry):
        value = tiles[slot_of[lax.div(position, lanes), lax.rem(position, lanes)]]
        rounded = value.astype(jnp.bfloat16)
        at_row = pl.multiple_of(lax.div(position, col_tiles) * tile, tile)
        at_col = pl.multiple_of(lax.rem(position, col_tiles) * tile, tile)
        high[pl.ds(at_row, tile), pl.ds(at_col, tile)] = rounded
        low[pl.ds(at_row, tile), pl.ds(at_col, tile)] = (
            value - rounded.astype(jnp.float32)
        ).astype(jnp.bfloat16)
        return carry

    tile_copy.wait()
    slot_copy.wait()
    for hop in range(1, reach + 1):

        @pl.when(exists(hop, 1))
        def _():
            pl.semaphore_wait(next_in.at[hop - 1], 1)

        if hop == 1 and deferred[1] == 1:
            send_own(0, 1, 1, jnp.logical_not(exists(2, 1)))
        elif hop <= reaches[1][0]:
            send_own(0, hop, 1)
        lax.fori_loop(
            positions * (hop - 1) // reach, positions * hop // reach, place, 0
        )
    own_copies[1].wait()
    small[2].wait()
    small[3].wait()
    row_index = lax.broadcasted_iota(jnp.int32, gap.shape, 0)
    energy = jnp.zeros(gap.shape, jnp.float32)
    for row in range(dest):
        energy = jnp.where(row_index == row, occ_energy[row], energy)
    gap[...] = virt_energy[...] - energy

    def relay(phase, distance, side):
        @pl.when(exists(distance, 1 - side) & exists(1, side))
        def _():
            which = o + distance * (1 - 2 * side)
            gather_copy(which, phase, 1, side).wait_recv()
            for hop in range(reaches[side][phase], 0, -1):

                @pl.when(exists(hop, side))
                def _():
                    gather_copy(which, phase, hop, side).start()

    def arrive(phase, distance):
        for side in range(2):
            here = exists(distance, 1 - side)
            if distance % reaches[side][phase] == 0 and distance < no - 1:
                here = here & jnp.logical_not(exists(1, side))

            @pl.when(here)
            def _():
                gather_copy(o + distance * (1 - 2 * side), phase, 1, side).wait_recv()

    def relays(wanted, sides):
        for distance in range(1, no - 1):
            for phase in wanted:
                for side in sides:
                    if distance % reaches[side][phase] == 0:
                        relay(phase, distance, side)

    relays([0], [1])
    for phase in range(1, phases):
        send_first(phase, 1)
    for phase in range(phases):
        for side in range(2):
            send_rest(phase, side)

    chunk = width // CHUNKS

    def split(phase):
        rows = lhss[phase].shape[0] // 2
        half = rows // 2
        level = levels[phase]
        if phase:
            for which in range(no):
                for pair in range(pairs):
                    for side in range(2):
                        stage[pl.ds(side * half + (which * pairs + pair) * level, level)] = amps[
                            phase
                        ][which, pair, pl.ds(side * level, level)]
        for side in range(2):
            if phase:
                value = stage[pl.ds(side * half, half)]
            else:
                value = amps[0][:, :, side].reshape(half, depth)
            rounded = value.astype(jnp.bfloat16)
            lhss[phase][pl.ds(side * half, half)] = rounded
            lhss[phase][pl.ds(rows + side * half, half)] = (
                value - rounded.astype(jnp.float32)
            ).astype(jnp.bfloat16)

    def core_copy(phase, at):
        cols = pl.ds(at * chunk, chunk)
        return pltpu.make_async_remote_copy(
            src_ref=parts[phase].at[1 - core, :, cols],
            dst_ref=partner_parts[phase].at[:, cols],
            send_sem=core_send.at[phase],
            recv_sem=core_recv.at[phase, at],
            device_id=other_core,
            device_id_type=MESH,
        )

    def chip_copy(phase, mask, at):
        cols = pl.ds(at * chunk, chunk)
        there = flip(chip, mask, chips)
        return pltpu.make_async_remote_copy(
            src_ref=summeds[phase].at[there, :, cols],
            dst_ref=arriveds[phase].at[mask - 1, :, cols],
            send_sem=chip_send.at[phase],
            recv_sem=chip_recv.at[phase],
            device_id=(o, 2 * there + core),
            device_id_type=MESH,
        )

    def every_core_copy(phase):
        return pltpu.make_async_remote_copy(
            src_ref=parts[phase].at[1 - core],
            dst_ref=partner_parts[phase],
            send_sem=core_send.at[phase],
            recv_sem=core_recv.at[phase, 0],
            device_id=other_core,
            device_id_type=MESH,
        )

    def every_chip_copy(phase):
        return pltpu.make_async_remote_copy(
            src_ref=summeds[phase].at[pl.ds(0, chips - 1)],
            dst_ref=arriveds[phase],
            send_sem=chip_send.at[phase],
            recv_sem=chip_recv.at[phase],
            device_id=other_core,
            device_id_type=MESH,
        )

    def multiply(phase, at):
        rows = lhss[phase].shape[0] // 2
        cols = pl.ds(at * chunk, chunk)
        wide = jnp.dot(lhss[phase][...], high[:, cols], preferred_element_type=jnp.float32)
        narrow = jnp.dot(
            lhss[phase][pl.ds(0, rows)], low[:, cols], preferred_element_type=jnp.float32
        )
        total = wide[:rows] + (wide[rows:] + narrow)
        parts[phase][:, :, cols] = total.reshape(2, rows // 2, chunk)
        core_copy(phase, at).start()

    def pass_on(phase, at):
        level = levels[phase]
        cols = pl.ds(at * chunk, chunk)
        core_copy(phase, at).wait_recv()
        for there in range(chips):
            rows = pl.ds(there * level, level)
            summeds[phase][there, :, cols] = (
                parts[phase][core, rows, cols] + partner_parts[phase][rows, cols]
            )
        for mask in range(chips - 1, 0, -1):
            chip_copy(phase, mask, at).start()

    relays([0], [0])
    relays(range(1, phases), [0, 1])
    for phase in range(phases):
        for distance in range(1, no):
            arrive(phase, distance)
        split(phase)
        if phase == 0:

            @pl.when(after > 0)
            def _():
                pl.semaphore_wait(plane_in, after)

        kept = KEEP if phase < phases - 1 else 0
        late = EARLY
        for at in range(CHUNKS + LAG):
            if at < CHUNKS:
                multiply(phase, at)
                if phase and at < KEEP:
                    pass_on(phase - 1, CHUNKS - KEEP + at)
            if late == LAG:
                if LAG <= at < CHUNKS + LAG - kept:
                    pass_on(phase, at - LAG)
            else:
                for which, lag in enumerate((late, LAG)):
                    if lag <= at < CHUNKS + lag - kept:

                        @pl.when(core == which)
                        def _():
                            pass_on(phase, at - lag)

    for phase in range(phases):
        for side in range(2):
            for distance in range(0, no, reaches[side][phase]):

                @pl.when(exists(distance, 1 - side))
                def _():
                    which = o + distance * (1 - 2 * side)
                    for hop in range(1, reaches[side][phase] + 1):

                        @pl.when(exists(hop, side))
                        def _():
                            gather_copy(which, phase, hop, side).wait_send()

    for phase in range(phases):
        rows = pl.ds(starts[phase], levels[phase])
        every_core_copy(phase).wait_send()
        every_chip_copy(phase).wait_recv()
        total = summeds[phase][chip]
        for mask in range(1, chips):
            total = total + arriveds[phase][mask - 1]
        out_ref[rows] = total / gap[rows]
        every_chip_copy(phase).wait_send()


def body(no, nv, amplitudes, tiles, tile_code, tile_count, occ_energy, virt_energy):
    block, depth = amplitudes.shape
    slots, tile, _ = tiles.shape
    width = virt_energy.shape[0]
    dest = occ_energy.shape[0]
    chips = nv // 2
    top = dest // 2
    levels = [top] + [(dest - top) // TAIL] * TAIL
    phases = len(levels)
    pairs = block // (2 * dest)
    close = no <= 4
    reaches = REACHES if close else ((1,) * phases,) * 2
    deferred = DEFER if close else (0, 0)
    reach = max(max(side) for side in reaches)
    map_shape = (max(8, (depth // tile) * (width // tile) // 128), 128)
    f32, bf16, i32 = jnp.float32, jnp.bfloat16, jnp.int32
    vmem, smem, dma = pltpu.VMEM, pltpu.SMEM, pltpu.SemaphoreType.DMA
    regular = pltpu.SemaphoreType.REGULAR
    return pl.pallas_call(
        functools.partial(kernel, no, nv, reaches, deferred),
        out_shape=jax.ShapeDtypeStruct((dest, width), f32),
        in_specs=[pl.BlockSpec(memory_space=pltpu.HBM)] * 6,
        out_specs=pl.BlockSpec(memory_space=pltpu.VMEM),
        scratch_shapes=[
            smem(tile_code.shape, i32),
            smem(tile_count.shape, i32),
            smem((dest,), f32),
            vmem((1, width), f32),
            vmem(map_shape, i32),
            smem(map_shape, i32),
            vmem((slots + 1, tile, tile), f32),
            vmem((depth, width), bf16),
            vmem((depth, width), bf16),
            [vmem((no, pairs, 2, top, depth), f32)]
            + [vmem((no, pairs, 2 * level, depth), f32) for level in levels[1:]],
            [vmem((4 * chips * level, depth), bf16) for level in levels],
            [vmem((2, chips * level, width), f32) for level in levels],
            [vmem((chips * level, width), f32) for level in levels],
            [vmem((chips, level, width), f32) for level in levels],
            [vmem((chips - 1, level, width), f32) for level in levels],
            vmem((pairs, 2, dest - top, depth), f32),
            vmem((2 * chips * levels[-1], depth), f32),
            vmem((dest, width), f32),
            dma((4,)),
            dma,
            dma,
            dma((2,)),
            regular((reach,)),
            regular,
            dma((2, no, reach, phases)),
            dma((no, phases)),
            dma((phases,)),
            dma((phases, CHUNKS)),
            dma((phases,)),
            dma((phases,)),
        ],
        compiler_params=pltpu.CompilerParams(
            collective_id=0, has_side_effects=True, vmem_limit_bytes=GRANT
        ),
    )(
        *(
            a if a is tile_count else pltpu.with_memory_space_constraint(a, pltpu.HBM)
            for a in (
                tile_code,
                tile_count,
                occ_energy,
                virt_energy.reshape(1, width),
                amplitudes.reshape(pairs, 2, 2, top, depth),
                tiles,
            )
        )
    )


def solution(mesh):
    placed = (
        P("occ", "virt"),
        P(("occ", "virt"), None, None),
        P(("occ", "virt")),
        P(("occ", "virt")),
        P("virt"),
        P("occ"),
    )
    return jax.shard_map(
        functools.partial(body, mesh.shape["occ"], mesh.shape["virt"]),
        mesh=mesh, in_specs=placed, out_specs=P("virt", "occ"), check_vma=False,
    )
```

```python
import functools

import jax
import jax.numpy as jnp
from jax import lax
from jax.experimental import pallas as pl
from jax.experimental.pallas import tpu as pltpu
from jax.sharding import PartitionSpec as P

MESH = pl.DeviceIdType.MESH
TAIL = 1
DEFER = (0, 2)
LAG = 2
EARLY = 0
KEEP = 1
CHUNKS = 4
REACHES = ((2, 2), (3, 2))
GRANT = 50 * 2**20


def flip(index, mask, size):
    out = index * 0
    bit = 1
    while bit < size:
        digit = lax.rem(lax.div(index, bit), 2)
        if mask & bit:
            digit = 1 - digit
        out = out + digit * bit
        bit *= 2
    return out


def kernel(
    no, nv, reaches, deferred,
    code_in, count_in, occ_in, virt_in, amp_in, tiles_in, out_ref,
    code, count, occ_energy, virt_energy, slot_map, slot_of,
    tiles, high, low, amps, lhss, parts, partner_parts, summeds, arriveds, own_tail, stage, gap,
    small_sem, slot_sem, tile_sem, own_sem, next_in, plane_in,
    gather_send, gather_recv, core_send, core_recv, chip_send, chip_recv,
):
    o = lax.axis_index("occ")
    v = lax.axis_index("virt")
    core = lax.rem(v, 2)
    chip = lax.div(v, 2)
    chips = nv // 2
    depth = amp_in.shape[-1]
    tile = tiles_in.shape[1]
    dest, width = out_ref.shape
    pairs = amp_in.shape[0]
    reach = max(max(side) for side in reaches)
    phases = len(amps)
    levels = [summed.shape[1] for summed in summeds]
    starts = [sum(levels[:phase]) for phase in range(phases)]
    col_tiles = width // tile
    positions = (depth // tile) * col_tiles
    slots = tiles_in.shape[0]
    other_core = (o, v + 1 - 2 * core)

    small = [
        pltpu.make_async_copy(source, target, small_sem.at[number])
        for number, (source, target) in enumerate(
            ((code_in, code), (count_in, count), (occ_in, occ_energy), (virt_in, virt_energy))
        )
    ]
    own_copies = [
        pltpu.make_async_copy(amp_in.at[:, :, 1], own_tail, own_sem.at[1]),
        pltpu.make_async_copy(amp_in.at[:, :, 0], amps[0].at[o], own_sem.at[0]),
    ]
    tile_copy = pltpu.make_async_copy(tiles_in, tiles.at[pl.ds(0, slots)], tile_sem)

    barrier = pltpu.get_barrier_semaphore()

    def meet(device):
        pl.semaphore_signal(barrier, inc=1, device_id=device, device_id_type=MESH)

    for hop in range(1, reach + 1):

        @pl.when(o + hop < no)
        def _():
            meet((o + hop, v))

    def one(condition):
        return condition.astype(jnp.int32)

    before = one(core == 1)
    after = one(core == 0)
    for mask in range(1, chips):
        there = flip(chip, mask, chips)
        before = before + one(there < chip)
        after = after + one(there > chip)

        @pl.when(there > chip)
        def _():
            meet((o, 2 * there + core))

    @pl.when(core == 0)
    def _():
        meet(other_core)

    own_copies[0].start()
    for copy in small:
        copy.start()
    own_copies[1].start()
    tile_copy.start()

    for hop in range(1, reach + 1):
        before = before + one(o >= hop)

    @pl.when(before > 0)
    def _():
        pl.semaphore_wait(barrier, before)

    for hop in range(1, reach + 1):

        @pl.when(o >= hop)
        def _():
            pl.semaphore_signal(
                next_in.at[hop - 1], inc=1, device_id=(o - hop, v), device_id_type=MESH
            )

    def gather_copy(which, phase, hop, side, source=None):
        held = amps[phase].at[which]
        return pltpu.make_async_remote_copy(
            src_ref=held if source is None else source,
            dst_ref=held,
            send_sem=gather_send.at[side, which, hop - 1, phase],
            recv_sem=gather_recv.at[which, phase],
            device_id=(o + hop * (2 * side - 1), v),
            device_id_type=MESH,
        )

    def exists(hop, side):
        return o + hop < no if side else o >= hop

    def send_own(phase, hop, side, wanted=True):
        @pl.when(exists(hop, side) & wanted)
        def _():
            gather_copy(o, phase, hop, side, amp_in.at[:, :, 0] if phase == 0 else None).start()

    def send_first(phase, side):
        for hop in range(reaches[side][phase], 0, -1):
            if hop == 1 and deferred[side] and phase >= deferred[side] - 1:
                send_own(phase, 1, side, jnp.logical_not(exists(2, side)))
            else:
                send_own(phase, hop, side)

    def send_rest(phase, side):
        if deferred[side] and phase >= deferred[side] - 1:
            send_own(phase, 1, side, exists(2, side))

    send_first(0, 0)

    for mask in range(1, chips):
        there = flip(chip, mask, chips)

        @pl.when(there < chip)
        def _():
            pl.semaphore_signal(
                plane_in, inc=1, device_id=(o, 2 * there + core), device_id_type=MESH
            )

    @pl.when(core == 1)
    def _():
        pl.semaphore_signal(plane_in, inc=1, device_id=other_core, device_id_type=MESH)

    own_copies[0].wait()
    for phase in range(1, phases):
        level = levels[phase]
        for pair in range(pairs):
            for side in range(2):
                amps[phase][o, pair, pl.ds(side * level, level)] = own_tail[
                    pair, side, pl.ds((phase - 1) * level, level)
                ]
    for phase in range(1, phases):
        send_first(phase, 0)

    tiles[slots] = jnp.zeros(tiles.shape[1:], tiles.dtype)
    small[0].wait()
    small[1].wait()
    lanes = slot_map.shape[1]
    place_index = lax.broadcasted_iota(jnp.int32, slot_map.shape, 0) * lanes + (
        lax.broadcasted_iota(jnp.int32, slot_map.shape, 1)
    )
    found = jnp.full(slot_map.shape, slots, jnp.int32)
    live = count[0]
    for slot in range(slots):
        found = jnp.where(place_index == jnp.where(slot < live, code[slot], -1), slot, found)
    slot_map[...] = found
    slot_copy = pltpu.make_async_copy(slot_map, slot_of, slot_sem)
    slot_copy.start()

    def place(position, carry):
        value = tiles[slot_of[lax.div(position, lanes), lax.rem(position, lanes)]]
        rounded = value.astype(jnp.bfloat16)
        at_row = pl.multiple_of(lax.div(position, col_tiles) * tile, tile)
        at_col = pl.multiple_of(lax.rem(position, col_tiles) * tile, tile)
        high[pl.ds(at_row, tile), pl.ds(at_col, tile)] = rounded
        low[pl.ds(at_row, tile), pl.ds(at_col, tile)] = (
            value - rounded.astype(jnp.float32)
        ).astype(jnp.bfloat16)
        return carry

    tile_copy.wait()
    slot_copy.wait()
    for hop in range(1, reach + 1):

        @pl.when(exists(hop, 1))
        def _():
            pl.semaphore_wait(next_in.at[hop - 1], 1)

        if hop == 1 and deferred[1] == 1:
            send_own(0, 1, 1, jnp.logical_not(exists(2, 1)))
        elif hop <= reaches[1][0]:
            send_own(0, hop, 1)
        lax.fori_loop(
            positions * (hop - 1) // reach, positions * hop // reach, place, 0
        )
    own_copies[1].wait()
    small[2].wait()
    small[3].wait()
    row_index = lax.broadcasted_iota(jnp.int32, gap.shape, 0)
    energy = jnp.zeros(gap.shape, jnp.float32)
    for row in range(dest):
        energy = jnp.where(row_index == row, occ_energy[row], energy)
    gap[...] = virt_energy[...] - energy

    def relay(phase, distance, side):
        @pl.when(exists(distance, 1 - side) & exists(1, side))
        def _():
            which = o + distance * (1 - 2 * side)
            gather_copy(which, phase, 1, side).wait_recv()
            for hop in range(reaches[side][phase], 0, -1):

                @pl.when(exists(hop, side))
                def _():
                    gather_copy(which, phase, hop, side).start()

    def arrive(phase, distance):
        for side in range(2):
            here = exists(distance, 1 - side)
            if distance % reaches[side][phase] == 0 and distance < no - 1:
                here = here & jnp.logical_not(exists(1, side))

            @pl.when(here)
            def _():
                gather_copy(o + distance * (1 - 2 * side), phase, 1, side).wait_recv()

    def relays(wanted, sides):
        for distance in range(1, no - 1):
            for phase in wanted:
                for side in sides:
                    if distance % reaches[side][phase] == 0:
                        relay(phase, distance, side)

    relays([0], [1])
    for phase in range(1, phases):
        send_first(phase, 1)
    for phase in range(phases):
        for side in range(2):
            send_rest(phase, side)

    chunk = width // CHUNKS

    def split(phase):
        rows = lhss[phase].shape[0] // 2
        half = rows // 2
        level = levels[phase]
        if phase:
            for which in range(no):
                for pair in range(pairs):
                    for side in range(2):
                        stage[pl.ds(side * half + (which * pairs + pair) * level, level)] = amps[
                            phase
                        ][which, pair, pl.ds(side * level, level)]
        for side in range(2):
            if phase:
                value = stage[pl.ds(side * half, half)]
            else:
                value = amps[0][:, :, side].reshape(half, depth)
            rounded = value.astype(jnp.bfloat16)
            lhss[phase][pl.ds(side * half, half)] = rounded
            lhss[phase][pl.ds(rows + side * half, half)] = (
                value - rounded.astype(jnp.float32)
            ).astype(jnp.bfloat16)

    def core_copy(phase, at):
        cols = pl.ds(at * chunk, chunk)
        return pltpu.make_async_remote_copy(
            src_ref=parts[phase].at[1 - core, :, cols],
            dst_ref=partner_parts[phase].at[:, cols],
            send_sem=core_send.at[phase],
            recv_sem=core_recv.at[phase, at],
            device_id=other_core,
            device_id_type=MESH,
        )

    def chip_copy(phase, mask, at):
        cols = pl.ds(at * chunk, chunk)
        there = flip(chip, mask, chips)
        return pltpu.make_async_remote_copy(
            src_ref=summeds[phase].at[there, :, cols],
            dst_ref=arriveds[phase].at[mask - 1, :, cols],
            send_sem=chip_send.at[phase],
            recv_sem=chip_recv.at[phase],
            device_id=(o, 2 * there + core),
            device_id_type=MESH,
        )

    def every_core_copy(phase):
        return pltpu.make_async_remote_copy(
            src_ref=parts[phase].at[1 - core],
            dst_ref=partner_parts[phase],
            send_sem=core_send.at[phase],
            recv_sem=core_recv.at[phase, 0],
            device_id=other_core,
            device_id_type=MESH,
        )

    def every_chip_copy(phase):
        return pltpu.make_async_remote_copy(
            src_ref=summeds[phase].at[pl.ds(0, chips - 1)],
            dst_ref=arriveds[phase],
            send_sem=chip_send.at[phase],
            recv_sem=chip_recv.at[phase],
            device_id=other_core,
            device_id_type=MESH,
        )

    def multiply(phase, at):
        rows = lhss[phase].shape[0] // 2
        cols = pl.ds(at * chunk, chunk)
        wide = jnp.dot(lhss[phase][...], high[:, cols], preferred_element_type=jnp.float32)
        narrow = jnp.dot(
            lhss[phase][pl.ds(0, rows)], low[:, cols], preferred_element_type=jnp.float32
        )
        total = wide[:rows] + (wide[rows:] + narrow)
        parts[phase][:, :, cols] = total.reshape(2, rows // 2, chunk)
        core_copy(phase, at).start()

    def pass_on(phase, at):
        level = levels[phase]
        cols = pl.ds(at * chunk, chunk)
        core_copy(phase, at).wait_recv()
        for there in range(chips):
            rows = pl.ds(there * level, level)
            summeds[phase][there, :, cols] = (
                parts[phase][core, rows, cols] + partner_parts[phase][rows, cols]
            )
        for mask in range(chips - 1, 0, -1):
            chip_copy(phase, mask, at).start()

    relays([0], [0])
    relays(range(1, phases), [0, 1])
    for phase in range(phases):
        for distance in range(1, no):
            arrive(phase, distance)
        split(phase)
        if phase == 0:

            @pl.when(after > 0)
            def _():
                pl.semaphore_wait(plane_in, after)

        kept = KEEP if phase < phases - 1 else 0
        late = EARLY
        for at in range(CHUNKS + LAG):
            if at < CHUNKS:
                multiply(phase, at)
                if phase and at < KEEP:

                    @pl.when(core == 1)
                    def _():
                        pass_on(phase - 1, CHUNKS - KEEP + at)

            if late == LAG:
                if LAG <= at < CHUNKS + LAG - kept:
                    pass_on(phase, at - LAG)
            else:
                for which, lag in enumerate((late, LAG)):
                    if lag <= at < CHUNKS + lag - kept * which:

                        @pl.when(core == which)
                        def _():
                            pass_on(phase, at - lag)

    for phase in range(phases):
        for side in range(2):
            for distance in range(0, no, reaches[side][phase]):

                @pl.when(exists(distance, 1 - side))
                def _():
                    which = o + distance * (1 - 2 * side)
                    for hop in range(1, reaches[side][phase] + 1):

                        @pl.when(exists(hop, side))
                        def _():
                            gather_copy(which, phase, hop, side).wait_send()

    for phase in range(phases):
        rows = pl.ds(starts[phase], levels[phase])
        every_core_copy(phase).wait_send()
        every_chip_copy(phase).wait_recv()
        total = summeds[phase][chip]
        for mask in range(1, chips):
            total = total + arriveds[phase][mask - 1]
        out_ref[rows] = total / gap[rows]
        every_chip_copy(phase).wait_send()


def body(no, nv, amplitudes, tiles, tile_code, tile_count, occ_energy, virt_energy):
    block, depth = amplitudes.shape
    slots, tile, _ = tiles.shape
    width = virt_energy.shape[0]
    dest = occ_energy.shape[0]
    chips = nv // 2
    top = dest // 2
    levels = [top] + [(dest - top) // TAIL] * TAIL
    phases = len(levels)
    pairs = block // (2 * dest)
    close = no <= 4
    reaches = REACHES if close else ((1,) * phases,) * 2
    deferred = DEFER if close else (0, 0)
    reach = max(max(side) for side in reaches)
    map_shape = (max(8, (depth // tile) * (width // tile) // 128), 128)
    f32, bf16, i32 = jnp.float32, jnp.bfloat16, jnp.int32
    vmem, smem, dma = pltpu.VMEM, pltpu.SMEM, pltpu.SemaphoreType.DMA
    regular = pltpu.SemaphoreType.REGULAR
    return pl.pallas_call(
        functools.partial(kernel, no, nv, reaches, deferred),
        out_shape=jax.ShapeDtypeStruct((dest, width), f32),
        in_specs=[pl.BlockSpec(memory_space=pltpu.HBM)] * 6,
        out_specs=pl.BlockSpec(memory_space=pltpu.VMEM),
        scratch_shapes=[
            smem(tile_code.shape, i32),
            smem(tile_count.shape, i32),
            smem((dest,), f32),
            vmem((1, width), f32),
            vmem(map_shape, i32),
            smem(map_shape, i32),
            vmem((slots + 1, tile, tile), f32),
            vmem((depth, width), bf16),
            vmem((depth, width), bf16),
            [vmem((no, pairs, 2, top, depth), f32)]
            + [vmem((no, pairs, 2 * level, depth), f32) for level in levels[1:]],
            [vmem((4 * chips * level, depth), bf16) for level in levels],
            [vmem((2, chips * level, width), f32) for level in levels],
            [vmem((chips * level, width), f32) for level in levels],
            [vmem((chips, level, width), f32) for level in levels],
            [vmem((chips - 1, level, width), f32) for level in levels],
            vmem((pairs, 2, dest - top, depth), f32),
            vmem((2 * chips * levels[-1], depth), f32),
            vmem((dest, width), f32),
            dma((4,)),
            dma,
            dma,
            dma((2,)),
            regular((reach,)),
            regular,
            dma((2, no, reach, phases)),
            dma((no, phases)),
            dma((phases,)),
            dma((phases, CHUNKS)),
            dma((phases,)),
            dma((phases,)),
        ],
        compiler_params=pltpu.CompilerParams(
            collective_id=0, has_side_effects=True, vmem_limit_bytes=GRANT
        ),
    )(
        *(
            a if a is tile_count else pltpu.with_memory_space_constraint(a, pltpu.HBM)
            for a in (
                tile_code,
                tile_count,
                occ_energy,
                virt_energy.reshape(1, width),
                amplitudes.reshape(pairs, 2, 2, top, depth),
                tiles,
            )
        )
    )


def solution(mesh):
    placed = (
        P("occ", "virt"),
        P(("occ", "virt"), None, None),
        P(("occ", "virt")),
        P(("occ", "virt")),
        P("virt"),
        P("occ"),
    )
    return jax.shard_map(
        functools.partial(body, mesh.shape["occ"], mesh.shape["virt"]),
        mesh=mesh, in_specs=placed, out_specs=P("virt", "occ"), check_vma=False,
    )
```
